32 devices in a mesh: grp: 2 (over y), col: 8 (over z, x), row: 2 (over core).
Axes of the slice: x: 2, y: 2, z: 4, core: 2. Of those that a mesh axis runs over, the one named last changes fastest.
Arguments:
- left_bounds: bfloat16 [4, 8, 128, 8, 128], P(('grp', 'row'), 'col'), parts along dimension 0, may hold values from -0.1875 to 0.1875
- right_bounds: bfloat16 [4, 8, 128, 8, 128], P(('grp', 'row'), 'col'), parts along dimension 0, may hold values from -0.1875 to 0.1875
- site_tensors: bfloat16 [4, 8, 2, 4096], P(('grp', 'row'), 'col'), parts along dimension 0, may hold values from -2 to 2
- configuration: int32 [4, 8], P(('grp', 'row'), 'col'), parts along dimension 0, may hold values from 0 to 1
- top_env: bfloat16 [16, 128, 8, 128], P(('grp', 'col')), parts along dimension 0, may hold values from -6 to 6
- bottom_env: bfloat16 [16, 128, 8, 128], P(('grp', 'col')), parts along dimension 0, may hold values from -6 to 6
- sketch: bfloat16 [1024, 128], replicated, may hold values from -0.1875 to 0.1875
Outputs:
- gradient: float32 [4, 8, 2, 4096], P(('grp', 'row'), 'col'), parts along dimension 0
- left_updated: bfloat16 [4, 8, 128, 8, 128], P(('grp', 'row'), 'col'), parts along dimension 0
- right_updated: bfloat16 [4, 8, 128, 8, 128], P(('grp', 'row'), 'col'), parts along dimension 0
The draws below stay inside these ranges and needn't reach their ends.
There are 2 independent parts, one for each index of `grp`. The reference program is written for one: setup_inputs(seed, part) draws one part's arguments, and reference() takes and returns one part's arrays. A program takes and returns all parts, laid end to end along the dimension named above; an argument that names none is the same for every part. Nothing has to cross between parts.
All inputs are finite; a program needn't handle non-finite values.
Results may differ from the reference program's by a relative error of at most 0.015.
Values may be sent and summed in bfloat16 or wider, within the bound.
A program may use at most 64 MiB of HBM per device.

```python
import math
import jax
import jax.numpy as jnp
from jax import lax

D = 8
PHYS = 2
CHI = 128
ROWS = 2
COLS = 8


def environment_field(key, noise, strength):
    row_key, col_key = jax.random.split(key, 2)
    row_part = jax.random.normal(row_key, (COLS, CHI, D, 1), jnp.float32)
    col_part = jax.random.normal(col_key, (COLS, 1, 1, CHI), jnp.float32)
    field = (noise + strength * row_part * col_part) / math.sqrt(1.0 + strength * strength)
    return jnp.clip(field, -6.0, 6.0).astype(jnp.bfloat16)


def environment_draw(key):
    noise_key, shared_key = jax.random.split(key, 2)
    noise = jax.random.normal(noise_key, (COLS, CHI, D, CHI), jnp.float32)
    strength = 1.2
    return environment_field(shared_key, noise, strength)


def draw_top_env(key, part):
    return environment_draw(jax.random.fold_in(key, 101))


def draw_bottom_env(key, part):
    return environment_draw(jax.random.fold_in(key, 202))


def set_ends(result, key, smallest, top_value):
    longest = result.shape.index(max(result.shape))
    spots = []
    for shift in (0, 1):
        where = [jax.random.randint(jax.random.fold_in(key, axis), (), 0, length) for axis, length in enumerate(result.shape)]
        where[longest] = (where[longest] + shift) % result.shape[longest]
        spots.append(tuple(where))
    return result.at[spots[0]].set(smallest).at[spots[1]].set(top_value)


def steps_of(rng, dims, shards, smallest, high):
    factor_of, own = 1.0, jax.random.fold_in(rng, 6)
    for axis_at, shards_of in shards:
        steps = jnp.exp(jax.random.uniform(jax.random.fold_in(own, axis_at), (shards_of,), jnp.float32, smallest / len(shards), high / len(shards)))
        factor_of = factor_of * jnp.repeat(steps, dims[axis_at] // shards_of).reshape([-1 if axis == axis_at else 1 for axis in range(len(dims))])
    return factor_of


def bell_draw(rng, extent, spread, limit, cuts=(), kind=jnp.bfloat16):
    drawn = spread * jax.random.normal(rng, extent, jnp.float32)
    if cuts:
        drawn = drawn * steps_of(rng, extent, cuts, -0.22, 0.18)
    return jnp.clip(drawn, -limit, limit).astype(kind)


def setup_inputs(seed: int = 0, part: int = 0) -> dict:
    key_of = jax.random.split(jax.random.key(seed), 8)
    part_keys = jax.random.split(jax.random.fold_in(key_of[7], part), 8)
    left_bounds = bell_draw(part_keys[0], (ROWS, COLS, CHI, D, CHI), (CHI * D) ** -0.5, 0.1875, ((0, 2), (1, 8)))
    right_bounds = bell_draw(part_keys[1], (ROWS, COLS, CHI, D, CHI), (CHI * D) ** -0.5, 0.1875, ((0, 2), (1, 8)))
    site_tensors = bell_draw(part_keys[2], (ROWS, COLS, PHYS, D**4), D ** -0.5, 2.0, ((0, 2), (1, 8)))
    configuration = set_ends(jax.random.randint(part_keys[3], (ROWS, COLS), 0, PHYS), jax.random.fold_in(part_keys[3], 1), 0, PHYS - 1).astype(jnp.int32)
    top_env = draw_top_env(jax.random.fold_in(jax.random.fold_in(key_of[7], part), 71), part)
    bottom_env = draw_bottom_env(jax.random.fold_in(jax.random.fold_in(key_of[7], part), 71), part)
    sketch = bell_draw(key_of[6], (CHI * D, CHI), (CHI * D) ** -0.5, 0.1875)
    return {"left_bounds": left_bounds, "right_bounds": right_bounds, "site_tensors": site_tensors, "configuration": configuration, "top_env": top_env, "bottom_env": bottom_env, "sketch": sketch}


def widen(array):
    return lax.optimization_barrier(array).astype(jnp.float32)

def orthonormal_basis(matrix):
    gram_matrix = jnp.dot(matrix.T.astype(jnp.float32), matrix.astype(jnp.float32), precision=lax.Precision.HIGHEST, preferred_element_type=jnp.float32)
    cholesky_factor = jnp.linalg.cholesky(gram_matrix)
    solved = lax.linalg.triangular_solve(cholesky_factor, matrix, left_side=False, lower=True, transpose_a=True)
    return solved.astype(jnp.bfloat16)

def project_row(frame_basis, boundary_row, oriented, sketch, closing):
    chi_size = boundary_row.shape[0]
    bond_size = boundary_row.shape[1]
    frame_tensor = widen(frame_basis).reshape(chi_size, bond_size, chi_size)
    partial_value = jnp.einsum('aup,akb->upkb', frame_tensor, widen(boundary_row)).astype(jnp.bfloat16)
    absorbed = jnp.einsum('upkb,kuod->pobd', widen(partial_value), widen(oriented)).astype(jnp.bfloat16)
    unfolded = widen(absorbed).reshape(chi_size * bond_size, chi_size * bond_size)
    if closing is None:
        closing = orthonormal_basis(jnp.dot(unfolded.T, widen(sketch)))
    unscaled = jnp.dot(unfolded, widen(closing))
    scaled = unscaled * lax.rsqrt(jnp.mean(unscaled * unscaled) + 1e-06)
    return (scaled.reshape(chi_size, bond_size, chi_size).astype(jnp.bfloat16), closing)

def pass_down(carried, western_row, core_row, eastern_row):
    partial_value = jnp.einsum('mun,mlb->unlb', widen(carried.astype(jnp.bfloat16)), widen(western_row)).astype(jnp.bfloat16)
    middle = jnp.einsum('unlb,luxd->nbxd', widen(partial_value), widen(core_row)).astype(jnp.bfloat16)
    return (partial_value, jnp.einsum('nbxd,nxc->bdc', widen(middle), widen(eastern_row)))

def pass_up(carried, western_row, core_row, eastern_row):
    lower_part = jnp.einsum('bdc,nxc->bdnx', widen(carried.astype(jnp.bfloat16)), widen(eastern_row)).astype(jnp.bfloat16)
    lower_mid = jnp.einsum('bdnx,luxd->bnlu', widen(lower_part), widen(core_row)).astype(jnp.bfloat16)
    return (lower_part, jnp.einsum('bnlu,mlb->mun', widen(lower_mid), widen(western_row)))

def reference(left_bounds, right_bounds, site_tensors, configuration, top_env, bottom_env, sketch):
    western_all = jnp.roll(left_bounds, 1, axis=1)
    eastern_all = jnp.roll(right_bounds, -1, axis=1)
    selection = jnp.arange(PHYS, dtype=jnp.int32)[None, None, :, None] == configuration[:, :, None, None]
    selected = lax.optimization_barrier(jnp.sum(jnp.where(selection, site_tensors, jnp.zeros_like(site_tensors)), axis=2))

    def column(packed):
        western, eastern, cores_flat, chooser, upper_edge, lower_edge = packed
        site_core = cores_flat.reshape(ROWS, D, D, D, D)
        mirrored = site_core.transpose(0, 3, 2, 1, 4)
        updated = []
        for boundary, oriented, upper, lower in ((western, site_core, upper_edge, lower_edge), (eastern, mirrored, upper_edge.transpose(2, 1, 0), lower_edge.transpose(2, 1, 0))):
            frame_basis = orthonormal_basis(upper.astype(jnp.float32).reshape(CHI * D, CHI))
            closing_edge = orthonormal_basis(lower.astype(jnp.float32).reshape(CHI * D, CHI))
            collected = []
            for position in range(ROWS):
                closing = closing_edge if position == ROWS - 1 else None
                new_row, frame_basis = project_row(frame_basis, boundary[position], oriented[position], sketch, closing)
                collected.append(new_row)
            updated.append(jnp.stack(collected))
        carried = upper_edge.astype(jnp.float32)
        partials = []
        for position in range(ROWS):
            partial_value, carried = pass_down(carried, western[position], site_core[position], eastern[position])
            partials.append(partial_value)
        carried = lower_edge.astype(jnp.float32)
        lowers = [None] * ROWS
        for position in reversed(range(ROWS)):
            lowers[position], carried = pass_up(carried, western[position], site_core[position], eastern[position])
        gradient_rows = jnp.stack([jnp.einsum('unlb,bdnx->luxd', widen(partials[position]), widen(lowers[position])).reshape(-1) for position in range(ROWS)])
        gradient = jnp.where(chooser, gradient_rows.reshape(ROWS, 1, D ** 4) * (D / CHI), 0.0)
        return (gradient, updated[0], updated[1])
    gradient, left_new, right_new = lax.map(column, (western_all.transpose(1, 0, 2, 3, 4), eastern_all.transpose(1, 0, 2, 3, 4), selected.transpose(1, 0, 2), selection.transpose(1, 0, 2, 3), top_env, bottom_env))
    return (gradient.transpose(1, 0, 2, 3), left_new.transpose(1, 0, 2, 3, 4), right_new.transpose(1, 0, 2, 3, 4))
```

```python
import jax
import jax.numpy as jnp
from jax import lax
from jax.experimental import pallas as pl
from jax.experimental.pallas import tpu as pltpu
from jax.sharding import PartitionSpec as P

HIGHEST = lax.Precision.HIGHEST
BLOCK = 8


def shift(value, axis, distance):
    count = lax.axis_size(axis)
    return lax.ppermute(value, axis, [(i, (i + distance) % count) for i in range(count)])


def dot(lhs, rhs, dims, precision=None):
    return lax.dot_general(
        lhs, rhs, (dims, ((), ())), precision=precision, preferred_element_type=jnp.float32
    )


def spread_row(value, row):
    return jnp.broadcast_to(value[row : row + 1, :], value.shape)


def eliminate_panel(rows, inverse, start):
    sublane = lax.broadcasted_iota(jnp.int32, rows.shape, 0)
    columns = [
        jnp.broadcast_to(rows[:, start + c : start + c + 1], rows.shape) for c in range(BLOCK)
    ]
    for c in range(BLOCK):
        scale = lax.rsqrt(spread_row(columns[c], c))
        factor = jnp.where(
            sublane > c, columns[c] * (scale * scale), jnp.where(sublane == c, 1.0 - scale, 0.0)
        )
        rows = rows - factor * spread_row(rows, c)
        inverse = inverse - factor * spread_row(inverse, c)
        for k in range(c + 1, BLOCK):
            columns[k] = columns[k] - factor * spread_row(columns[k], c)
    return rows, inverse


def inverse_factors(grams):
    size = grams[0].shape[0]
    ones = (
        lax.broadcasted_iota(jnp.int32, (size, size), 0)
        == lax.broadcasted_iota(jnp.int32, (size, size), 1)
    ).astype(jnp.float32)
    states = [jnp.concatenate([gram, ones], axis=1) for gram in grams]
    found = [[] for _ in grams]
    for start in range(0, size, BLOCK):
        for q in range(len(grams)):
            rows, inverse = eliminate_panel(
                states[q][:BLOCK, :size], states[q][:BLOCK, size:], start
            )
            found[q].append(inverse)
            if start + BLOCK < size:
                update = dot(
                    rows, jnp.concatenate([rows, inverse], axis=1), ((0,), (0,)), HIGHEST
                )
                states[q] = states[q][BLOCK:] - update[start + BLOCK :]
    return [jnp.concatenate(blocks, axis=0) for blocks in found]


def apply_transposed(matrix, inverse):
    if matrix.dtype == jnp.float32:
        return dot(matrix, inverse, ((1,), (1,)), HIGHEST)
    high = inverse.astype(jnp.bfloat16)
    rest = inverse - high.astype(jnp.float32)
    middle = rest.astype(jnp.bfloat16)
    low = (rest - middle.astype(jnp.float32)).astype(jnp.bfloat16)
    total = dot(matrix, low, ((1,), (1,)))
    total = total + dot(matrix, middle, ((1,), (1,)))
    return total + dot(matrix, high, ((1,), (1,)))


def basis_kernel(left_ref, right_ref, left_out, right_out):
    grams = []
    for ref in (left_ref, right_ref):
        matrix = ref[...]
        precision = HIGHEST if matrix.dtype == jnp.float32 else None
        grams.append(dot(matrix, matrix, ((0,), (0,)), precision))
    inverses = inverse_factors(grams)
    for ref, out, inverse in zip((left_ref, right_ref), (left_out, right_out), inverses):
        out[...] = apply_transposed(ref[...], inverse).astype(jnp.bfloat16)


def orthonormal_pair(left, right):
    shape = jax.ShapeDtypeStruct(left.shape, jnp.bfloat16)
    return pl.pallas_call(
        basis_kernel,
        out_shape=(shape, shape),
        in_specs=[pl.BlockSpec(memory_space=pltpu.VMEM)] * 2,
        out_specs=(pl.BlockSpec(memory_space=pltpu.VMEM),) * 2,
        compiler_params=pltpu.CompilerParams(vmem_limit_bytes=32 * 1024 * 1024),
        cost_estimate=pl.CostEstimate(
            flops=2_000_000_000, bytes_accessed=2_000_000, transcendentals=0
        ),
    )(left, right)


def contract(spec, lhs, rhs):
    return jnp.einsum(spec, lhs, rhs, preferred_element_type=jnp.float32)


def half(value):
    return value.astype(jnp.bfloat16)


def normalized(unscaled):
    return half(unscaled * lax.rsqrt(jnp.mean(unscaled * unscaled) + 1e-06))


def local(left_bounds, right_bounds, site_tensors, configuration, top_env, bottom_env, sketch):
    chi = left_bounds.shape[2]
    bond = left_bounds.shape[3]
    phys = site_tensors.shape[2]
    cube = (chi, bond, chi)
    leading = lax.axis_index("row") == 0
    western = shift(left_bounds, "col", 1)[0, 0]
    eastern = shift(right_bounds, "col", -1)[0, 0]
    selection = (
        lax.broadcasted_iota(jnp.int32, (1, 1, phys, 1), 2) == configuration[:, :, None, None]
    )
    selected = jnp.sum(jnp.where(selection, site_tensors, jnp.zeros_like(site_tensors)), axis=2)
    core = selected.reshape(bond, bond, bond, bond)
    downward = [(0, 1)]
    western_0 = lax.ppermute(western, "row", downward)
    eastern_0 = lax.ppermute(eastern, "row", downward)
    core_0 = lax.ppermute(selected.reshape(-1), "row", downward).reshape(core.shape)
    mirrored = core.transpose(2, 1, 0, 3)
    env = jnp.where(leading, top_env[0], bottom_env[0])
    base_left, base_right = orthonormal_pair(
        env.reshape(chi * bond, chi), env.transpose(2, 1, 0).reshape(chi * bond, chi)
    )

    def upper():
        bulk = []
        sketched = []
        for base, boundary, oriented in (
            (base_left, western, core),
            (base_right, eastern, mirrored),
        ):
            partial = half(contract("aup,akb->upkb", base.reshape(cube), boundary))
            absorbed = half(contract("upkb,kuod->podb", partial, oriented))
            bulk.append(absorbed)
            sketched.append(
                contract("podb,poe->bde", absorbed, sketch.reshape(cube)).reshape(
                    chi * bond, chi
                )
            )
        next_left, next_right = orthonormal_pair(*sketched)
        blank = jnp.zeros((bond, bond, bond, bond), jnp.float32)
        return next_left, next_right, bulk[0], bulk[1], blank, blank

    def lower():
        bulk = []
        for base, boundary, oriented in (
            (base_left, western, core),
            (base_right, eastern, mirrored),
        ):
            joined = half(contract("akb,bde->adke", boundary, base.reshape(cube)))
            bulk.append(half(contract("adke,kuod->auoe", joined, oriented)))
        part_0 = half(contract("mun,mlb->unlb", top_env[0], western_0))
        middle = half(contract("unlb,luxd->nxdb", part_0, core_0))
        state = half(contract("nxdb,nxc->bdc", middle, eastern_0))
        part_1 = half(contract("mun,mlb->unlb", state, western))
        key_1 = half(contract("bdc,nxc->dnxb", bottom_env[0], eastern))
        low = half(contract("dnxb,luxd->nlub", key_1, core))
        state = half(contract("nlub,mlb->mun", low, western))
        key_0 = half(contract("bdc,nxc->dnxb", state, eastern_0))
        grads = [
            contract("unlb,dnxb->luxd", part, key)
            for part, key in ((part_0, key_0), (part_1, key_1))
        ]
        blank = jnp.zeros((chi * bond, chi), jnp.bfloat16)
        return blank, blank, bulk[0], bulk[1], grads[0], grads[1]

    next_left, next_right, bulk_left, bulk_right, grad_0, grad_1 = lax.cond(
        leading, upper, lower
    )
    sent_left = lax.ppermute(next_left, "row", downward)
    sent_right = lax.ppermute(next_right, "row", downward)
    grad_sent = lax.ppermute(grad_0, "row", [(1, 0)])

    def upper_end():
        return tuple(
            normalized(contract("podb,bde->poe", bulk, basis.reshape(cube)))
            for bulk, basis in ((bulk_left, next_left), (bulk_right, next_right))
        )

    def lower_end():
        return tuple(
            normalized(contract("aup,auoe->poe", basis.reshape(cube), bulk))
            for bulk, basis in ((bulk_left, sent_left), (bulk_right, sent_right))
        )

    left_new, right_new = lax.cond(leading, upper_end, lower_end)
    gradient = jnp.where(leading, grad_sent, grad_1).reshape(1, 1, 1, bond**4)
    gradient = jnp.where(selection, gradient * (bond / chi), 0.0)
    return gradient, left_new[None, None], right_new[None, None]


def solution(mesh):
    return jax.shard_map(
        local,
        mesh=mesh,
        in_specs=(
            P(("grp", "row"), "col", None, None, None),
            P(("grp", "row"), "col", None, None, None),
            P(("grp", "row"), "col", None, None),
            P(("grp", "row"), "col"),
            P(("grp", "col"), None, None, None),
            P(("grp", "col"), None, None, None),
            P(),
        ),
        out_specs=(
            P(("grp", "row"), "col", None, None),
            P(("grp", "row"), "col", None, None, None),
            P(("grp", "row"), "col", None, None, None),
        ),
        check_vma=False,
    )
```

```python
import jax
import jax.numpy as jnp
from jax import lax
from jax.experimental import pallas as pl
from jax.experimental.pallas import tpu as pltpu
from jax.sharding import PartitionSpec as P

HIGHEST = lax.Precision.HIGHEST
BLOCK = 8


def shift(value, axis, distance):
    count = lax.axis_size(axis)
    return lax.ppermute(value, axis, [(i, (i + distance) % count) for i in range(count)])


def shift_down(value, distance):
    count, rows = lax.axis_size("col"), lax.axis_size("row")
    route = [(i * rows, (i + distance) % count * rows + 1) for i in range(count)]
    return lax.ppermute(value, ("col", "row"), route)


def dot(lhs, rhs, dims, precision=None):
    return lax.dot_general(
        lhs, rhs, (dims, ((), ())), precision=precision, preferred_element_type=jnp.float32
    )


def spread_row(value, row):
    return jnp.broadcast_to(value[row : row + 1, :], value.shape)


def eliminate_panel(rows, inverse, start):
    sublane = lax.broadcasted_iota(jnp.int32, rows.shape, 0)
    columns = [
        jnp.broadcast_to(rows[:, start + c : start + c + 1], rows.shape) for c in range(BLOCK)
    ]
    for c in range(BLOCK):
        scale = lax.rsqrt(spread_row(columns[c], c))
        factor = jnp.where(
            sublane > c, columns[c] * (scale * scale), jnp.where(sublane == c, 1.0 - scale, 0.0)
        )
        rows = rows - factor * spread_row(rows, c)
        inverse = inverse - factor * spread_row(inverse, c)
        for k in range(c + 1, BLOCK):
            columns[k] = columns[k] - factor * spread_row(columns[k], c)
    return rows, inverse


def inverse_factors(grams):
    size = grams[0].shape[0]
    ones = (
        lax.broadcasted_iota(jnp.int32, (size, size), 0)
        == lax.broadcasted_iota(jnp.int32, (size, size), 1)
    ).astype(jnp.float32)
    states = [jnp.concatenate([gram, ones], axis=1) for gram in grams]
    found = [[] for _ in grams]
    for start in range(0, size, BLOCK):
        for q in range(len(grams)):
            rows, inverse = eliminate_panel(
                states[q][:BLOCK, :size], states[q][:BLOCK, size:], start
            )
            found[q].append(inverse)
            if start + BLOCK < size:
                update = dot(
                    rows, jnp.concatenate([rows, inverse], axis=1), ((0,), (0,)), HIGHEST
                )
                states[q] = states[q][BLOCK:] - update[start + BLOCK :]
    return [jnp.concatenate(blocks, axis=0) for blocks in found]


def apply_transposed(matrix, inverse):
    if matrix.dtype == jnp.float32:
        return dot(matrix, inverse, ((1,), (1,)), HIGHEST)
    high = inverse.astype(jnp.bfloat16)
    rest = inverse - high.astype(jnp.float32)
    middle = rest.astype(jnp.bfloat16)
    low = (rest - middle.astype(jnp.float32)).astype(jnp.bfloat16)
    total = dot(matrix, low, ((1,), (1,)))
    total = total + dot(matrix, middle, ((1,), (1,)))
    return total + dot(matrix, high, ((1,), (1,)))


BF16 = jnp.bfloat16


def half(value):
    return value.astype(BF16)


def flat(ref):
    outer, inner, lane = ref.shape
    return ref.reshape(outer * inner, lane)


def split_legs(matrix, rows_ref, count):
    size = rows_ref.shape[0] // count
    rows_ref[...] = matrix.astype(jnp.float32)
    return [half(rows_ref[pl.ds(leg, size, stride=count), :]) for leg in range(count)]


def project(planes, boundary, target):
    count = len(planes)
    size = planes[0].shape[1]
    rows = flat(target)
    for u in range(count):
        product = dot(planes[u], boundary, ((0,), (0,)))
        for k in range(count):
            rows[pl.ds(u * count + k, size, stride=count * count), :] = product[
                :, k * size : (k + 1) * size
            ]


def pair_up(matrix, others, dims, target):
    outer, inner, lane = target.shape
    bond = matrix.shape[0] // outer
    product = dot(matrix, others, dims)
    for d in range(bond):
        target[:, d * bond : (d + 1) * bond, :] = product[:, d * lane : (d + 1) * lane].reshape(
            outer, bond, lane
        )


def mix(weights, source, store):
    outer, inner, lane = source.shape
    rows = flat(source)
    group = 8

    def step(i, carry):
        blocks = []
        for j in range(group):
            begin = pl.multiple_of((i * group + j) * inner, inner)
            blocks.append(half(rows[pl.ds(begin, inner), :]))
        product = dot(weights, jnp.concatenate(blocks, axis=1), ((1,), (0,)))
        for j in range(group):
            store(i * group + j, product[:, j * lane : (j + 1) * lane])
        return carry

    lax.fori_loop(0, outer // group, step, 0)


def store_natural(target):
    inner = target.shape[1]
    rows = flat(target)

    def store(index, block):
        rows[pl.ds(pl.multiple_of(index * inner, inner), inner), :] = block

    return store


def store_by_leg(target, bond):
    length = target.shape[0] * bond
    rows = flat(target)

    def store(index, block):
        for d in range(bond):
            begin = pl.multiple_of(d * length + index * bond, bond)
            rows[pl.ds(begin, bond), :] = block[d * bond : (d + 1) * bond]

    return store


def leg_block(source, d, bond):
    length = source.shape[0] * bond
    return half(flat(source)[pl.ds(d * length, length), :])


def joined(planes):
    return jnp.concatenate(planes, axis=1)


def edge_kernel(env_ref, left_out, right_out, rows_ref):
    bond = env_ref.shape[0] // env_ref.shape[1]
    planes = split_legs(env_ref[...], rows_ref, bond)
    left = jnp.concatenate(planes, axis=0)
    right = jnp.concatenate([plane.T for plane in planes], axis=0)
    grams = [dot(matrix, matrix, ((0,), (0,))) for matrix in (left, right)]
    inverses = inverse_factors(grams)
    left_out[...] = half(apply_transposed(left, inverses[0]))
    right_out[...] = half(apply_transposed(right, inverses[1]))


def upper_kernel(
    left_base, right_base, west_ref, east_ref, left_mix, right_mix, sketch_ref,
    left_next, right_next, left_bulk, right_bulk, rows_ref, part_ref, absorbed_ref,
):
    size = west_ref.shape[1]
    bond = west_ref.shape[0] // size
    sketched = []
    for base, boundary, weights, bulk in (
        (left_base, west_ref, left_mix, left_bulk),
        (right_base, east_ref, right_mix, right_bulk),
    ):
        legs = joined(split_legs(boundary[...], rows_ref, bond))
        planes = [base[u * size : (u + 1) * size, :] for u in range(bond)]
        project(planes, legs, part_ref)
        mix(weights[...], part_ref, store_by_leg(absorbed_ref, bond))
        parts = []
        for d in range(bond):
            block = leg_block(absorbed_ref, d, bond)
            bulk[:, d * size : (d + 1) * size] = block
            parts.append(dot(block, sketch_ref[...], ((0,), (0,))))
        sketched.append(jnp.concatenate(parts, axis=0))
    grams = [dot(matrix, matrix, ((0,), (0,)), HIGHEST) for matrix in sketched]
    inverses = inverse_factors(grams)
    left_next[...] = half(apply_transposed(sketched[0], inverses[0]))
    right_next[...] = half(apply_transposed(sketched[1], inverses[1]))


def lower_kernel(
    left_edge, right_edge, west_ref, east_ref, left_mix, right_mix,
    top_ref, bottom_ref, west_above, east_above, down_mix,
    left_bulk, right_bulk, grad_above, grad_here,
    rows_ref, first_ref, second_ref, third_ref, mixed_ref,
):
    size = west_ref.shape[1]
    bond = west_ref.shape[0] // size
    steps = bond * bond
    for edge, boundary, weights, bulk in (
        (left_edge, west_ref, left_mix, left_bulk),
        (right_edge, east_ref, right_mix, right_bulk),
    ):
        blocks = joined([edge[d * size : (d + 1) * size, :] for d in range(bond)])
        pair_up(boundary[...], blocks, ((1,), (0,)), first_ref)
        mix(weights[...], first_ref, store_natural(mixed_ref))
        for u in range(bond):
            for o in range(bond):
                bulk[u * size : (u + 1) * size, o * size : (o + 1) * size] = half(
                    flat(mixed_ref)[pl.ds(u * bond + o, size, stride=steps), :]
                )
    west_0 = joined(split_legs(west_above[...], rows_ref, bond))
    west_1 = joined(split_legs(west_ref[...], rows_ref, bond))
    project(split_legs(top_ref[...], rows_ref, bond), west_0, first_ref)
    mix(down_mix[...], first_ref, store_by_leg(mixed_ref, bond))
    state = [
        half(dot(leg_block(mixed_ref, d, bond), east_above[...], ((0,), (0,))))
        for d in range(bond)
    ]
    project(state, west_1, third_ref)
    state = jnp.concatenate(split_legs(bottom_ref[...], rows_ref, bond), axis=0)
    pair_up(east_ref[...], state, ((1,), (1,)), second_ref)
    mix(right_mix[...], second_ref, store_natural(mixed_ref))
    overlap(third_ref, second_ref, grad_here)
    lows = []
    for u in range(bond):
        low = joined(
            [
                half(flat(mixed_ref)[pl.ds(u * bond + k, size, stride=steps), :])
                for k in range(bond)
            ]
        )
        lows.append(half(dot(west_1, low, ((1,), (1,)))))
    pair_up(east_above[...], jnp.concatenate(lows, axis=0), ((1,), (1,)), second_ref)
    overlap(first_ref, second_ref, grad_above)


def overlap(part_ref, key_ref, out_ref):
    outer, inner, lane = part_ref.shape
    group = 8

    def gather(ref, i):
        rows = flat(ref)
        return joined(
            [
                half(rows[pl.ds(pl.multiple_of((i * group + j) * inner, inner), inner), :])
                for j in range(group)
            ]
        )

    def step(i, total):
        return total + dot(gather(part_ref, i), gather(key_ref, i), ((1,), (1,)))

    out_ref[...] = lax.fori_loop(
        0, outer // group, step, jnp.zeros((inner, inner), jnp.float32)
    )


def normalized(unscaled):
    mean = jnp.sum(unscaled * unscaled, keepdims=True) * (1.0 / unscaled.size)
    return unscaled * lax.rsqrt(mean + 1e-06)


def upper_end_kernel(left_bulk, right_bulk, left_basis, right_basis, left_out, right_out):
    for bulk, basis, out in (
        (left_bulk, left_basis, left_out),
        (right_bulk, right_basis, right_out),
    ):
        out[...] = half(normalized(dot(bulk[...], basis[...], ((1,), (0,)))))


def lower_end_kernel(
    left_bulk, right_bulk, left_basis, right_basis, left_out, right_out, rows_ref
):
    for bulk, basis, out in (
        (left_bulk, left_basis, left_out),
        (right_bulk, right_basis, right_out),
    ):
        size = basis.shape[1]
        bond = basis.shape[0] // size
        scaled = normalized(dot(basis[...], bulk[...], ((0,), (0,))))
        for o in range(bond):
            rows_ref[pl.ds(o, size, stride=bond), :] = scaled[:, o * size : (o + 1) * size]
        out[...] = half(rows_ref[...])


def run(kernel, outs, scratch, flops, *args):
    in_vmem = pl.BlockSpec(memory_space=pltpu.VMEM)
    return pl.pallas_call(
        kernel,
        out_shape=tuple(jax.ShapeDtypeStruct(shape, kind) for shape, kind in outs),
        in_specs=[in_vmem] * len(args),
        out_specs=(in_vmem,) * len(outs),
        scratch_shapes=[pltpu.VMEM(shape, jnp.float32) for shape in scratch],
        compiler_params=pltpu.CompilerParams(vmem_limit_bytes=48 * 1024 * 1024),
        cost_estimate=pl.CostEstimate(
            flops=flops, bytes_accessed=2_000_000, transcendentals=0
        ),
    )(*args)


def local(left_bounds, right_bounds, site_tensors, configuration, top_env, bottom_env, sketch):
    chi = left_bounds.shape[2]
    bond = left_bounds.shape[3]
    phys = site_tensors.shape[2]
    tall = (chi * bond, chi)
    wide = (chi * bond, chi * bond)
    square = (bond * bond, bond * bond)
    volume = (chi, bond * bond, chi)
    row = lax.axis_index("row")
    leading = row == 0
    left_flat = left_bounds.reshape(tall)
    right_flat = right_bounds.reshape(tall)
    western = shift(left_flat, "col", 1)
    eastern = shift(right_flat, "col", -1)
    western_0 = shift_down(left_flat, 1)
    eastern_0 = shift_down(right_flat, -1)
    selection = (
        lax.broadcasted_iota(jnp.int32, (1, 1, phys, 1), 2) == configuration[:, :, None, None]
    )
    selected = jnp.sum(jnp.where(selection, site_tensors, jnp.zeros_like(site_tensors)), axis=2)
    core = selected.reshape(bond, bond, bond, bond)
    core_0 = lax.ppermute(selected.reshape(-1), "row", [(0, 1)]).reshape(core.shape)
    env = jnp.where(leading, top_env[0], bottom_env[0]).reshape(tall)
    base_left, base_right = run(
        edge_kernel, [(tall, BF16)] * 2, [tall], 10_000_000_000, env
    )

    def upper():
        next_left, next_right, bulk_left, bulk_right = run(
            upper_kernel,
            [(tall, BF16)] * 2 + [(wide, BF16)] * 2,
            [tall, volume, volume],
            10_000_000_000,
            base_left,
            base_right,
            western,
            eastern,
            core.transpose(3, 2, 1, 0).reshape(square),
            core.transpose(3, 0, 1, 2).reshape(square),
            sketch,
        )
        blank = jnp.zeros(square, jnp.float32)
        return next_left, next_right, bulk_left, bulk_right, blank, blank

    def lower():
        bulk_left, bulk_right, grad_0, grad_1 = run(
            lower_kernel,
            [(wide, BF16)] * 2 + [(square, jnp.float32)] * 2,
            [tall, volume, volume, volume, volume],
            10_000_000_000,
            base_left,
            base_right,
            western,
            eastern,
            core.transpose(1, 2, 3, 0).reshape(square),
            core.transpose(1, 0, 3, 2).reshape(square),
            top_env.reshape(tall),
            bottom_env.reshape(tall),
            western_0,
            eastern_0,
            core_0.transpose(3, 2, 1, 0).reshape(square),
        )
        blank = jnp.zeros(tall, BF16)
        return blank, blank, bulk_left, bulk_right, grad_0, grad_1

    next_left, next_right, bulk_left, bulk_right, grad_0, grad_1 = lax.cond(
        leading, upper, lower
    )
    sent_left = lax.ppermute(next_left, "row", [(0, 1)])
    sent_right = lax.ppermute(next_right, "row", [(0, 1)])
    grad_sent = lax.ppermute(grad_0, "row", [(1, 0)])

    def upper_end():
        return run(
            upper_end_kernel, [(tall, BF16)] * 2, [], 1_000_000_000,
            bulk_left, bulk_right, next_left, next_right,
        )

    def lower_end():
        return run(
            lower_end_kernel, [(tall, BF16)] * 2, [tall], 1_000_000_000,
            bulk_left, bulk_right, sent_left, sent_right,
        )

    left_new, right_new = lax.cond(leading, upper_end, lower_end)
    gradient = jnp.where(leading, grad_sent, grad_1).reshape(bond, bond, bond, bond)
    gradient = gradient.transpose(1, 0, 3, 2).reshape(1, 1, 1, bond**4)
    gradient = jnp.where(selection, gradient * (bond / chi), 0.0)
    return (
        gradient,
        left_new.reshape(left_bounds.shape),
        right_new.reshape(right_bounds.shape),
    )


def solution(mesh):
    return jax.shard_map(
        local,
        mesh=mesh,
        in_specs=(
            P(("grp", "row"), "col", None, None, None),
            P(("grp", "row"), "col", None, None, None),
            P(("grp", "row"), "col", None, None),
            P(("grp", "row"), "col"),
            P(("grp", "col"), None, None, None),
            P(("grp", "col"), None, None, None),
            P(),
        ),
        out_specs=(
            P(("grp", "row"), "col", None, None),
            P(("grp", "row"), "col", None, None, None),
            P(("grp", "row"), "col", None, None, None),
        ),
        check_vma=False,
    )
```

```python
import jax
import jax.numpy as jnp
from jax import lax
from jax.experimental import pallas as pl
from jax.experimental.pallas import tpu as pltpu
from jax.sharding import PartitionSpec as P

HIGHEST = lax.Precision.HIGHEST
BLOCK = 8


def shift(value, axis, distance):
    count = lax.axis_size(axis)
    return lax.ppermute(value, axis, [(i, (i + distance) % count) for i in range(count)])


def shift_down(value, distance):
    count, rows = lax.axis_size("col"), lax.axis_size("row")
    route = [(i * rows, (i + distance) % count * rows + 1) for i in range(count)]
    return lax.ppermute(value, ("col", "row"), route)


def dot(lhs, rhs, dims, precision=None):
    return lax.dot_general(
        lhs, rhs, (dims, ((), ())), precision=precision, preferred_element_type=jnp.float32
    )


def spread_row(value, row):
    return jnp.broadcast_to(value[row : row + 1, :], value.shape)


def eliminate_panel(rows, start):
    size = rows.shape[1] // 2
    shape = (BLOCK, size)
    sublane = lax.broadcasted_iota(jnp.int32, shape, 0)
    turned = pltpu.roll(rows[:, :size], size - start, axis=1)
    columns = [jnp.broadcast_to(turned[:, c : c + 1], shape) for c in range(BLOCK)]
    halves = [rows[:, :size], rows[:, size:]]
    for c in range(BLOCK):
        scale = lax.rsqrt(spread_row(columns[c], c))
        factor = jnp.where(
            sublane > c, columns[c] * (scale * scale), jnp.where(sublane == c, 1.0 - scale, 0.0)
        )
        halves = [value - factor * spread_row(value, c) for value in halves]
        for k in range(c + 1, BLOCK):
            columns[k] = columns[k] - factor * spread_row(columns[k], c)
    return halves


def inverse_factors(grams, state):
    size = grams[0].shape[0]
    ones = (
        lax.broadcasted_iota(jnp.int32, (size, size), 0)
        == lax.broadcasted_iota(jnp.int32, (size, size), 1)
    ).astype(jnp.float32)
    for q, gram in enumerate(grams):
        state[q, :, :size] = gram
        state[q, :, size:] = ones
    lane = lax.broadcasted_iota(jnp.int32, (BLOCK, size), 1)

    def step(i, carry):
        start = pl.multiple_of(i * BLOCK, BLOCK)
        for q in range(len(grams)):
            rows, inverse = eliminate_panel(state[q, pl.ds(start, BLOCK), :], start)
            below = jnp.where(lane >= start + BLOCK, rows, 0.0)
            solved = jnp.concatenate([rows, inverse], axis=1)
            state[q] = state[q] - dot(below, solved, ((0,), (0,)), HIGHEST)
            state[q, pl.ds(start, BLOCK), :] = solved
        return carry

    lax.fori_loop(0, size // BLOCK, step, 0)
    return [state[q, :, size:] for q in range(len(grams))]


def row_block(i, size):
    return pl.ds(pl.multiple_of(i * size, size), size)


def gram_of(source, size):
    precision = HIGHEST if source.dtype == jnp.float32 else None

    def step(i, total):
        block = source[row_block(i, size), :]
        return total + dot(block, block, ((0,), (0,)), precision)

    start = jnp.zeros((size, size), jnp.float32)
    return lax.fori_loop(0, source.shape[0] // size, step, start)


def apply_transposed(source, inverse, out):
    size = inverse.shape[0]
    if source.dtype == jnp.float32:

        def step(i, carry):
            block = dot(source[row_block(i, size), :], inverse, ((1,), (1,)), HIGHEST)
            out[row_block(i, size), :] = block.astype(jnp.bfloat16)
            return carry

    else:
        high = inverse.astype(jnp.bfloat16)
        rest = inverse - high.astype(jnp.float32)
        middle = rest.astype(jnp.bfloat16)
        low = (rest - middle.astype(jnp.float32)).astype(jnp.bfloat16)

        def step(i, carry):
            block = source[row_block(i, size), :]
            total = dot(block, low, ((1,), (1,)))
            total = total + dot(block, middle, ((1,), (1,)))
            total = total + dot(block, high, ((1,), (1,)))
            out[row_block(i, size), :] = total.astype(jnp.bfloat16)
            return carry

    lax.fori_loop(0, source.shape[0] // size, step, 0)


BF16 = jnp.bfloat16
F32 = jnp.float32


def half(value):
    return value.astype(BF16)


def flat(ref):
    outer, inner, lane = ref.shape
    return ref.reshape(outer * inner, lane)


def split_legs(matrix, rows_ref, count):
    size = rows_ref.shape[0] // count
    rows_ref[...] = matrix.astype(jnp.float32)
    return [half(rows_ref[pl.ds(leg, size, stride=count), :]) for leg in range(count)]


def stack(planes, target):
    size = planes[0].shape[0]
    for i, plane in enumerate(planes):
        target[i * size : (i + 1) * size, :] = plane


def project(planes, boundary, target):
    size = planes.shape[1]
    count = planes.shape[0] // size
    rows = flat(target)

    def step(u, carry):
        product = dot(planes[row_block(u, size), :], boundary, ((0,), (0,)))
        for k in range(count):
            rows[pl.ds(u * count + k, size, stride=count * count), :] = product[
                :, k * size : (k + 1) * size
            ]
        return carry

    lax.fori_loop(0, count, step, 0)


def pair_up(matrix, others, swap, target):
    outer, inner, lane = target.shape
    bond = matrix.shape[0] // outer
    dims = ((1,), (1,)) if swap else ((1,), (0,))
    left = matrix[...]

    def step(d, carry):
        product = dot(left, others[row_block(d, lane), :], dims)
        target[:, row_block(d, bond), :] = product.reshape(outer, bond, lane)
        return carry

    lax.fori_loop(0, bond, step, 0)


def mix(weights, source, store):
    outer, inner, lane = source.shape
    rows = flat(source)
    group = 8

    def step(i, carry):
        blocks = []
        for j in range(group):
            begin = pl.multiple_of((i * group + j) * inner, inner)
            blocks.append(half(rows[pl.ds(begin, inner), :]))
        product = dot(weights, jnp.concatenate(blocks, axis=1), ((1,), (0,)))
        for j in range(group):
            store(i * group + j, product[:, j * lane : (j + 1) * lane])
        return carry

    lax.fori_loop(0, outer // group, step, 0)


def store_natural(target):
    inner = target.shape[1]
    rows = flat(target)

    def store(index, block):
        rows[pl.ds(pl.multiple_of(index * inner, inner), inner), :] = block

    return store


def store_by_leg(target, bond):
    length = target.shape[0] * bond
    rows = flat(target)

    def store(index, block):
        for d in range(bond):
            begin = pl.multiple_of(d * length + index * bond, bond)
            rows[pl.ds(begin, bond), :] = block[d * bond : (d + 1) * bond]

    return store


def leg_block(source, d, bond):
    length = source.shape[0] * bond
    return half(flat(source)[row_block(d, length), :])


def joined(planes):
    return jnp.concatenate(planes, axis=1)


def edge_kernel(env_ref, left_out, right_out, rows_ref, left_ref, right_ref, state_ref):
    size = env_ref.shape[1]
    planes = split_legs(env_ref[...], rows_ref, env_ref.shape[0] // size)
    stack(planes, left_ref)
    stack([plane.T for plane in planes], right_ref)
    inverses = inverse_factors([gram_of(left_ref, size), gram_of(right_ref, size)], state_ref)
    apply_transposed(left_ref, inverses[0], left_out)
    apply_transposed(right_ref, inverses[1], right_out)


def upper_kernel(
    left_base, right_base, west_ref, east_ref, left_mix, right_mix, sketch_ref,
    left_next, right_next, left_bulk, right_bulk,
    rows_ref, part_ref, absorbed_ref, left_sum, right_sum, state_ref,
):
    size = west_ref.shape[1]
    bond = west_ref.shape[0] // size
    for base, boundary, weights, bulk, total in (
        (left_base, west_ref, left_mix, left_bulk, left_sum),
        (right_base, east_ref, right_mix, right_bulk, right_sum),
    ):
        project(base, joined(split_legs(boundary[...], rows_ref, bond)), part_ref)
        mix(weights[...], part_ref, store_by_leg(absorbed_ref, bond))

        def step(d, carry, bulk=bulk, total=total):
            block = leg_block(absorbed_ref, d, bond)
            bulk[d] = block
            total[row_block(d, size), :] = dot(block, sketch_ref[...], ((0,), (0,)))
            return carry

        lax.fori_loop(0, bond, step, 0)
    inverses = inverse_factors([gram_of(left_sum, size), gram_of(right_sum, size)], state_ref)
    apply_transposed(left_sum, inverses[0], left_next)
    apply_transposed(right_sum, inverses[1], right_next)


def lower_kernel(
    left_edge, right_edge, west_ref, east_ref, left_mix, right_mix,
    top_ref, bottom_ref, west_above, east_above, down_mix,
    left_bulk, right_bulk, grad_above, grad_here,
    rows_ref, first_ref, second_ref, third_ref, mixed_ref, state_ref,
):
    size = west_ref.shape[1]
    bond = west_ref.shape[0] // size
    steps = bond * bond
    for edge, boundary, weights, bulk in (
        (left_edge, west_ref, left_mix, left_bulk),
        (right_edge, east_ref, right_mix, right_bulk),
    ):
        pair_up(boundary, edge, False, first_ref)
        mix(weights[...], first_ref, store_natural(mixed_ref))

        def step(o, carry, bulk=bulk):
            for u in range(bond):
                bulk[o, u * size : (u + 1) * size, :] = half(
                    flat(mixed_ref)[pl.ds(u * bond + o, size, stride=steps), :]
                )
            return carry

        lax.fori_loop(0, bond, step, 0)
    west_0 = joined(split_legs(west_above[...], rows_ref, bond))
    west_1 = joined(split_legs(west_ref[...], rows_ref, bond))
    stack(split_legs(top_ref[...], rows_ref, bond), state_ref)
    project(state_ref, west_0, first_ref)
    mix(down_mix[...], first_ref, store_by_leg(mixed_ref, bond))

    def down(d, carry):
        block = leg_block(mixed_ref, d, bond)
        state_ref[row_block(d, size), :] = half(dot(block, east_above[...], ((0,), (0,))))
        return carry

    lax.fori_loop(0, bond, down, 0)
    project(state_ref, west_1, third_ref)
    stack(split_legs(bottom_ref[...], rows_ref, bond), state_ref)
    pair_up(east_ref, state_ref, True, second_ref)
    mix(right_mix[...], second_ref, store_natural(mixed_ref))
    overlap(third_ref, second_ref, grad_here)

    def up(u, carry):
        low = joined(
            [
                half(flat(mixed_ref)[pl.ds(u * bond + k, size, stride=steps), :])
                for k in range(bond)
            ]
        )
        state_ref[row_block(u, size), :] = half(dot(west_1, low, ((1,), (1,))))
        return carry

    lax.fori_loop(0, bond, up, 0)
    pair_up(east_above, state_ref, True, second_ref)
    overlap(first_ref, second_ref, grad_above)


def overlap(part_ref, key_ref, out_ref):
    outer, inner, lane = part_ref.shape
    group = 8

    def gather(ref, i):
        rows = flat(ref)
        return joined(
            [
                half(rows[pl.ds(pl.multiple_of((i * group + j) * inner, inner), inner), :])
                for j in range(group)
            ]
        )

    def step(i, total):
        return total + dot(gather(part_ref, i), gather(key_ref, i), ((1,), (1,)))

    out_ref[...] = lax.fori_loop(
        0, outer // group, step, jnp.zeros((inner, inner), jnp.float32)
    )


def upper_end_kernel(
    left_bulk, right_bulk, left_basis, right_basis, left_out, right_out, rows_ref
):
    for bulk, basis, out in (
        (left_bulk, left_basis, left_out),
        (right_bulk, right_basis, right_out),
    ):
        bond, length, size = bulk.shape

        def step(i, total, bulk=bulk, basis=basis):
            rows = row_block(i, size)
            block = dot(
                joined([bulk[d, rows, :] for d in range(bond)]), basis[...], ((1,), (0,))
            )
            rows_ref[rows, :] = block
            return total + jnp.sum(block * block, axis=0, keepdims=True)

        scaled_out(lax.fori_loop(0, length // size, step, jnp.zeros((1, size))), rows_ref, out)


def scaled_out(total, rows_ref, out):
    mean = jnp.sum(total, keepdims=True) * (1.0 / (rows_ref.shape[0] * rows_ref.shape[1]))
    out[...] = half(rows_ref[...] * lax.rsqrt(mean + 1e-06))


def lower_end_kernel(
    left_bulk, right_bulk, left_basis, right_basis, left_out, right_out, rows_ref
):
    for bulk, basis, out in (
        (left_bulk, left_basis, left_out),
        (right_bulk, right_basis, right_out),
    ):
        bond, length, size = bulk.shape
        flipped = basis[...].T

        def step(o, total, bulk=bulk, flipped=flipped):
            block = dot(flipped, bulk[o], ((1,), (0,)))
            rows_ref[pl.ds(o, size, stride=bond), :] = block
            return total + jnp.sum(block * block, axis=0, keepdims=True)

        scaled_out(lax.fori_loop(0, bond, step, jnp.zeros((1, size))), rows_ref, out)


def run(kernel, outs, scratch, flops, *args):
    in_vmem = pl.BlockSpec(memory_space=pltpu.VMEM)
    return pl.pallas_call(
        kernel,
        out_shape=tuple(jax.ShapeDtypeStruct(shape, kind) for shape, kind in outs),
        in_specs=[in_vmem] * len(args),
        out_specs=(in_vmem,) * len(outs),
        scratch_shapes=[pltpu.VMEM(shape, kind) for shape, kind in scratch],
        compiler_params=pltpu.CompilerParams(vmem_limit_bytes=48 * 1024 * 1024),
        cost_estimate=pl.CostEstimate(
            flops=flops, bytes_accessed=2_000_000, transcendentals=0
        ),
    )(*args)


def local(left_bounds, right_bounds, site_tensors, configuration, top_env, bottom_env, sketch):
    chi = left_bounds.shape[2]
    bond = left_bounds.shape[3]
    phys = site_tensors.shape[2]
    tall = (chi * bond, chi)
    wide = (bond, chi * bond, chi)
    pair = (2, chi, 2 * chi)
    square = (bond * bond, bond * bond)
    volume = (chi, bond * bond, chi)
    row = lax.axis_index("row")
    leading = row == 0
    left_flat = left_bounds.reshape(tall)
    right_flat = right_bounds.reshape(tall)
    western = shift(left_flat, "col", 1)
    eastern = shift(right_flat, "col", -1)
    western_0 = shift_down(left_flat, 1)
    eastern_0 = shift_down(right_flat, -1)
    selection = (
        lax.broadcasted_iota(jnp.int32, (1, 1, phys, 1), 2) == configuration[:, :, None, None]
    )
    selected = jnp.sum(jnp.where(selection, site_tensors, jnp.zeros_like(site_tensors)), axis=2)
    core = selected.reshape(bond, bond, bond, bond)
    core_0 = lax.ppermute(selected.reshape(-1), "row", [(0, 1)]).reshape(core.shape)
    env = jnp.where(leading, top_env[0], bottom_env[0]).reshape(tall)
    base_left, base_right = run(
        edge_kernel,
        [(tall, BF16)] * 2,
        [(tall, F32), (tall, BF16), (tall, BF16), (pair, F32)],
        10_000_000_000,
        env,
    )

    def upper():
        next_left, next_right, bulk_left, bulk_right = run(
            upper_kernel,
            [(tall, BF16)] * 2 + [(wide, BF16)] * 2,
            [(tall, F32), (volume, F32), (volume, F32), (tall, F32), (tall, F32), (pair, F32)],
            10_000_000_000,
            base_left,
            base_right,
            western,
            eastern,
            core.transpose(3, 2, 1, 0).reshape(square),
            core.transpose(3, 0, 1, 2).reshape(square),
            sketch,
        )
        blank = jnp.zeros(square, jnp.float32)
        return next_left, next_right, bulk_left, bulk_right, blank, blank

    def lower():
        bulk_left, bulk_right, grad_0, grad_1 = run(
            lower_kernel,
            [(wide, BF16)] * 2 + [(square, jnp.float32)] * 2,
            [(tall, F32)] + [(volume, F32)] * 4 + [(tall, BF16)],
            10_000_000_000,
            base_left,
            base_right,
            western,
            eastern,
            core.transpose(1, 2, 3, 0).reshape(square),
            core.transpose(1, 0, 3, 2).reshape(square),
            top_env.reshape(tall),
            bottom_env.reshape(tall),
            western_0,
            eastern_0,
            core_0.transpose(3, 2, 1, 0).reshape(square),
        )
        blank = jnp.zeros(tall, BF16)
        return blank, blank, bulk_left, bulk_right, grad_0, grad_1

    next_left, next_right, bulk_left, bulk_right, grad_0, grad_1 = lax.cond(
        leading, upper, lower
    )
    sent_left = lax.ppermute(next_left, "row", [(0, 1)])
    sent_right = lax.ppermute(next_right, "row", [(0, 1)])
    grad_sent = lax.ppermute(grad_0, "row", [(1, 0)])

    def upper_end():
        return run(
            upper_end_kernel, [(tall, BF16)] * 2, [(tall, F32)], 1_000_000_000,
            bulk_left, bulk_right, next_left, next_right,
        )

    def lower_end():
        return run(
            lower_end_kernel, [(tall, BF16)] * 2, [(tall, F32)], 1_000_000_000,
            bulk_left, bulk_right, sent_left, sent_right,
        )

    left_new, right_new = lax.cond(leading, upper_end, lower_end)
    gradient = jnp.where(leading, grad_sent, grad_1).reshape(bond, bond, bond, bond)
    gradient = gradient.transpose(1, 0, 3, 2).reshape(1, 1, 1, bond**4)
    gradient = jnp.where(selection, gradient * (bond / chi), 0.0)
    return (
        gradient,
        left_new.reshape(left_bounds.shape),
        right_new.reshape(right_bounds.shape),
    )


def solution(mesh):
    return jax.shard_map(
        local,
        mesh=mesh,
        in_specs=(
            P(("grp", "row"), "col", None, None, None),
            P(("grp", "row"), "col", None, None, None),
            P(("grp", "row"), "col", None, None),
            P(("grp", "row"), "col"),
            P(("grp", "col"), None, None, None),
            P(("grp", "col"), None, None, None),
            P(),
        ),
        out_specs=(
            P(("grp", "row"), "col", None, None),
            P(("grp", "row"), "col", None, None, None),
            P(("grp", "row"), "col", None, None, None),
        ),
        check_vma=False,
    )
```

```python
import jax
import jax.numpy as jnp
from jax import lax
from jax.experimental import pallas as pl
from jax.experimental.pallas import tpu as pltpu
from jax.sharding import PartitionSpec as P

HIGHEST = lax.Precision.HIGHEST
BLOCK = 8


def shift(value, axis, distance):
    count = lax.axis_size(axis)
    return lax.ppermute(value, axis, [(i, (i + distance) % count) for i in range(count)])


def dot(lhs, rhs, dims, precision=None):
    return lax.dot_general(
        lhs, rhs, (dims, ((), ())), precision=precision, preferred_element_type=jnp.float32
    )


def spread_row(value, row):
    return jnp.broadcast_to(value[row : row + 1, :], value.shape)


def eliminate_panel(rows, inverse, start):
    sublane = lax.broadcasted_iota(jnp.int32, rows.shape, 0)
    columns = [
        jnp.broadcast_to(rows[:, start + c : start + c + 1], rows.shape) for c in range(BLOCK)
    ]
    for c in range(BLOCK):
        scale = lax.rsqrt(spread_row(columns[c], c))
        factor = jnp.where(
            sublane > c, columns[c] * (scale * scale), jnp.where(sublane == c, 1.0 - scale, 0.0)
        )
        rows = rows - factor * spread_row(rows, c)
        inverse = inverse - factor * spread_row(inverse, c)
        for k in range(c + 1, BLOCK):
            columns[k] = columns[k] - factor * spread_row(columns[k], c)
    return rows, inverse


def inverse_factors(grams):
    size = grams[0].shape[0]
    ones = (
        lax.broadcasted_iota(jnp.int32, (size, size), 0)
        == lax.broadcasted_iota(jnp.int32, (size, size), 1)
    ).astype(jnp.float32)
    states = [jnp.concatenate([gram, ones], axis=1) for gram in grams]
    found = [[] for _ in grams]
    for start in range(0, size, BLOCK):
        for q in range(len(grams)):
            rows, inverse = eliminate_panel(
                states[q][:BLOCK, :size], states[q][:BLOCK, size:], start
            )
            found[q].append(inverse)
            if start + BLOCK < size:
                update = dot(
                    rows, jnp.concatenate([rows, inverse], axis=1), ((0,), (0,)), HIGHEST
                )
                states[q] = states[q][BLOCK:] - update[start + BLOCK :]
    return [jnp.concatenate(blocks, axis=0) for blocks in found]


def loop(count, step, start=0, unroll=2):
    def several(i, carry):
        for j in range(unroll):
            carry = step(i * unroll + j, carry)
        return carry

    return lax.fori_loop(0, count // unroll, several, start)


def row_block(i, size):
    return pl.ds(pl.multiple_of(i * size, size), size)


def gram_of(source, size):
    precision = HIGHEST if source.dtype == jnp.float32 else None

    def step(i, total):
        block = source[row_block(i, size), :]
        return total + dot(block, block, ((0,), (0,)), precision)

    start = jnp.zeros((size, size), jnp.float32)
    return loop(source.shape[0] // size, step, start)


def apply_transposed(source, inverse, out):
    size = inverse.shape[0]
    if source.dtype == jnp.float32:

        def step(i, carry):
            block = dot(source[row_block(i, size), :], inverse, ((1,), (1,)), HIGHEST)
            out[row_block(i, size), :] = block.astype(jnp.bfloat16)
            return carry

    else:
        high = inverse.astype(jnp.bfloat16)
        rest = inverse - high.astype(jnp.float32)
        middle = rest.astype(jnp.bfloat16)
        low = (rest - middle.astype(jnp.float32)).astype(jnp.bfloat16)

        def step(i, carry):
            block = source[row_block(i, size), :]
            total = dot(block, low, ((1,), (1,)))
            total = total + dot(block, middle, ((1,), (1,)))
            total = total + dot(block, high, ((1,), (1,)))
            out[row_block(i, size), :] = total.astype(jnp.bfloat16)
            return carry

    loop(source.shape[0] // size, step)


BF16 = jnp.bfloat16
F32 = jnp.float32


def half(value):
    return value.astype(BF16)


def flat(ref):
    outer, inner, lane = ref.shape
    return ref.reshape(outer * inner, lane)


def split_legs(matrix, rows_ref, count):
    size = rows_ref.shape[0] // count
    rows_ref[...] = matrix.astype(jnp.float32)
    return [half(rows_ref[pl.ds(leg, size, stride=count), :]) for leg in range(count)]


def stack(planes, target):
    size = planes[0].shape[0]
    for i, plane in enumerate(planes):
        target[i * size : (i + 1) * size, :] = plane


def project(planes, boundary, target):
    size = planes.shape[1]
    count = planes.shape[0] // size
    rows = flat(target)

    def step(u, carry):
        product = dot(planes[row_block(u, size), :], boundary, ((0,), (0,)))
        for k in range(count):
            rows[pl.ds(u * count + k, size, stride=count * count), :] = product[
                :, k * size : (k + 1) * size
            ]
        return carry

    loop(count, step)


def pair_up(matrix, others, swap, target):
    outer, inner, lane = target.shape
    bond = matrix.shape[0] // outer
    dims = ((1,), (1,)) if swap else ((1,), (0,))
    left = matrix[...]

    def step(d, carry):
        product = dot(left, others[row_block(d, lane), :], dims)
        target[:, row_block(d, bond), :] = product.reshape(outer, bond, lane)
        return carry

    loop(bond, step)


def mix(weights, source, store):
    outer, inner, lane = source.shape
    rows = flat(source)
    group = 8

    def step(i, carry):
        blocks = []
        for j in range(group):
            begin = pl.multiple_of((i * group + j) * inner, inner)
            blocks.append(half(rows[pl.ds(begin, inner), :]))
        product = dot(weights, jnp.concatenate(blocks, axis=1), ((1,), (0,)))
        for j in range(group):
            store(i * group + j, product[:, j * lane : (j + 1) * lane])
        return carry

    loop(outer // group, step)


def store_natural(target):
    inner = target.shape[1]
    rows = flat(target)

    def store(index, block):
        rows[pl.ds(pl.multiple_of(index * inner, inner), inner), :] = block

    return store


def store_by_leg(target, bond):
    length = target.shape[0] * bond
    rows = flat(target)

    def store(index, block):
        for d in range(bond):
            begin = pl.multiple_of(d * length + index * bond, bond)
            rows[pl.ds(begin, bond), :] = block[d * bond : (d + 1) * bond]

    return store


def leg_block(source, d, bond):
    length = source.shape[0] * bond
    return half(flat(source)[row_block(d, length), :])


def joined(planes):
    return jnp.concatenate(planes, axis=1)


def edge_kernel(env_ref, left_out, right_out, rows_ref, left_ref, right_ref):
    size = env_ref.shape[1]
    planes = split_legs(env_ref[...], rows_ref, env_ref.shape[0] // size)
    stack(planes, left_ref)
    stack([plane.T for plane in planes], right_ref)
    inverses = inverse_factors([gram_of(left_ref, size), gram_of(right_ref, size)])
    apply_transposed(left_ref, inverses[0], left_out)
    apply_transposed(right_ref, inverses[1], right_out)


def upper_kernel(
    left_base, right_base, west_ref, east_ref, left_mix, right_mix, sketch_ref,
    next_ref, left_bulk, right_bulk, rows_ref, part_ref, absorbed_ref, left_sum, right_sum,
):
    size = west_ref.shape[1]
    bond = west_ref.shape[0] // size
    for base, boundary, weights, bulk, total in (
        (left_base, west_ref, left_mix, left_bulk, left_sum),
        (right_base, east_ref, right_mix, right_bulk, right_sum),
    ):
        project(base, joined(split_legs(boundary[...], rows_ref, bond)), part_ref)
        mix(weights[...], part_ref, store_by_leg(absorbed_ref, bond))

        def step(d, carry, bulk=bulk, total=total):
            block = leg_block(absorbed_ref, d, bond)
            bulk[d] = block
            total[row_block(d, size), :] = dot(block, sketch_ref[...], ((0,), (0,)))
            return carry

        loop(bond, step)
    inverses = inverse_factors([gram_of(left_sum, size), gram_of(right_sum, size)])
    length = left_sum.shape[0]
    apply_transposed(left_sum, inverses[0], next_ref.at[:length])
    apply_transposed(right_sum, inverses[1], next_ref.at[length:])


def lower_kernel(
    left_edge, right_edge, west_ref, east_ref, left_mix, right_mix,
    left_bulk, right_bulk, first_ref, mixed_ref,
):
    size = west_ref.shape[1]
    bond = west_ref.shape[0] // size
    steps = bond * bond
    for edge, boundary, weights, bulk in (
        (left_edge, west_ref, left_mix, left_bulk),
        (right_edge, east_ref, right_mix, right_bulk),
    ):
        pair_up(boundary, edge, False, first_ref)
        mix(weights[...], first_ref, store_natural(mixed_ref))

        def step(o, carry, bulk=bulk):
            for u in range(bond):
                bulk[o, u * size : (u + 1) * size, :] = half(
                    flat(mixed_ref)[pl.ds(u * bond + o, size, stride=steps), :]
                )
            return carry

        loop(bond, step)


def down_kernel(
    env_ref, west_ref, east_ref, weights, kept_ref, state_ref,
    rows_ref, planes_ref, first_ref, mixed_ref,
):
    size = west_ref.shape[1]
    bond = west_ref.shape[0] // size
    west = joined(split_legs(west_ref[...], rows_ref, bond))
    stack(split_legs(env_ref[...], rows_ref, bond), planes_ref)
    project(planes_ref, west, first_ref)
    mix(weights[...], first_ref, store_by_leg(mixed_ref, bond))
    kept_ref[...] = half(first_ref[...])

    def down(d, carry):
        block = leg_block(mixed_ref, d, bond)
        state_ref[row_block(d, size), :] = half(dot(block, east_ref[...], ((0,), (0,))))
        return carry

    loop(bond, down)


def up_kernel(
    env_ref, west_ref, east_ref, weights, kept_ref, state_ref,
    rows_ref, planes_ref, second_ref, mixed_ref,
):
    size = west_ref.shape[1]
    bond = west_ref.shape[0] // size
    west = joined(split_legs(west_ref[...], rows_ref, bond))
    stack(split_legs(env_ref[...], rows_ref, bond), planes_ref)
    pair_up(east_ref, planes_ref, True, second_ref)
    mix(weights[...], second_ref, store_natural(mixed_ref))
    kept_ref[...] = half(second_ref[...])

    def up(u, carry):
        low = joined(
            [
                half(flat(mixed_ref)[pl.ds(u * bond + k, size, stride=bond * bond), :])
                for k in range(bond)
            ]
        )
        state_ref[row_block(u, size), :] = half(dot(west, low, ((1,), (1,))))
        return carry

    loop(bond, up)


def upper_gradient(state_ref, east_ref, kept_ref, out_ref, volume_ref):
    pair_up(east_ref, state_ref, True, volume_ref)
    overlap(kept_ref, volume_ref, out_ref)


def lower_gradient(state_ref, west_ref, kept_ref, out_ref, rows_ref, volume_ref):
    bond = west_ref.shape[0] // west_ref.shape[1]
    project(state_ref, joined(split_legs(west_ref[...], rows_ref, bond)), volume_ref)
    overlap(volume_ref, kept_ref, out_ref)


def overlap(part_ref, key_ref, out_ref):
    outer, inner, lane = part_ref.shape
    group = 8

    def gather(ref, i):
        rows = flat(ref)
        return joined(
            [
                half(rows[pl.ds(pl.multiple_of((i * group + j) * inner, inner), inner), :])
                for j in range(group)
            ]
        )

    def step(i, total):
        return total + dot(gather(part_ref, i), gather(key_ref, i), ((1,), (1,)))

    out_ref[...] = lax.fori_loop(
        0, outer // group, step, jnp.zeros((inner, inner), jnp.float32)
    )


def upper_end_kernel(
    left_bulk, right_bulk, basis_ref, left_out, right_out, rows_ref
):
    for bulk, basis, out in (
        (left_bulk, basis_ref.at[: basis_ref.shape[0] // 2], left_out),
        (right_bulk, basis_ref.at[basis_ref.shape[0] // 2 :], right_out),
    ):
        bond, length, size = bulk.shape

        def step(i, total, bulk=bulk, basis=basis):
            rows = row_block(i, size)
            block = dot(
                joined([bulk[d, rows, :] for d in range(bond)]), basis[...], ((1,), (0,))
            )
            rows_ref[rows, :] = block
            return total + jnp.sum(block * block, axis=0, keepdims=True)

        scaled_out(loop(length // size, step, jnp.zeros((1, size))), rows_ref, out)


def scaled_out(total, rows_ref, out):
    mean = jnp.sum(total, keepdims=True) * (1.0 / (rows_ref.shape[0] * rows_ref.shape[1]))
    out[...] = half(rows_ref[...] * lax.rsqrt(mean + 1e-06))


def lower_end_kernel(
    left_bulk, right_bulk, basis_ref, left_out, right_out, rows_ref
):
    for bulk, basis, out in (
        (left_bulk, basis_ref.at[: basis_ref.shape[0] // 2], left_out),
        (right_bulk, basis_ref.at[basis_ref.shape[0] // 2 :], right_out),
    ):
        bond, length, size = bulk.shape
        flipped = basis[...].T

        def step(o, total, bulk=bulk, flipped=flipped):
            block = dot(flipped, bulk[o], ((1,), (0,)))
            rows_ref[pl.ds(o, size, stride=bond), :] = block
            return total + jnp.sum(block * block, axis=0, keepdims=True)

        scaled_out(loop(bond, step, jnp.zeros((1, size))), rows_ref, out)


def run(kernel, outs, scratch, flops, *args):
    in_vmem = pl.BlockSpec(memory_space=pltpu.VMEM)
    return pl.pallas_call(
        kernel,
        out_shape=tuple(jax.ShapeDtypeStruct(shape, kind) for shape, kind in outs),
        in_specs=[in_vmem] * len(args),
        out_specs=(in_vmem,) * len(outs),
        scratch_shapes=[pltpu.VMEM(shape, kind) for shape, kind in scratch],
        compiler_params=pltpu.CompilerParams(vmem_limit_bytes=48 * 1024 * 1024),
        cost_estimate=pl.CostEstimate(
            flops=flops, bytes_accessed=2_000_000, transcendentals=0
        ),
    )(*args)


def local(left_bounds, right_bounds, site_tensors, configuration, top_env, bottom_env, sketch):
    chi = left_bounds.shape[2]
    bond = left_bounds.shape[3]
    phys = site_tensors.shape[2]
    tall = (chi * bond, chi)
    wide = (bond, chi * bond, chi)
    double = (2 * chi * bond, chi)
    square = (bond * bond, bond * bond)
    volume = (chi, bond * bond, chi)
    row = lax.axis_index("row")
    leading = row == 0
    western = shift(left_bounds.reshape(tall), "col", 1)
    eastern = shift(right_bounds.reshape(tall), "col", -1)
    selection = (
        lax.broadcasted_iota(jnp.int32, (1, 1, phys, 1), 2) == configuration[:, :, None, None]
    )
    selected = jnp.sum(jnp.where(selection, site_tensors, jnp.zeros_like(site_tensors)), axis=2)
    core = selected.reshape(bond, bond, bond, bond)
    env = jnp.where(leading, top_env[0], bottom_env[0]).reshape(tall)
    base_left, base_right = run(
        edge_kernel,
        [(tall, BF16)] * 2,
        [(tall, F32), (tall, BF16), (tall, BF16)],
        10_000_000_000,
        env,
    )
    left_mix, right_mix = (
        jnp.where(leading, core.transpose(above), core.transpose(below)).reshape(square)
        for above, below in (((3, 2, 1, 0), (1, 2, 3, 0)), ((3, 0, 1, 2), (1, 0, 3, 2)))
    )

    def first_pass(kernel, weights):
        return lambda: run(
            kernel,
            [(volume, BF16), (tall, BF16)],
            [(tall, F32), (tall, BF16), (volume, F32), (volume, F32)],
            10_000_000_000,
            env,
            western,
            eastern,
            weights,
        )

    kept, state = lax.cond(
        leading, first_pass(down_kernel, left_mix), first_pass(up_kernel, right_mix)
    )
    received = lax.ppermute(state, "row", [(0, 1), (1, 0)])

    def upper():
        return run(
            upper_kernel,
            [(double, BF16)] + [(wide, BF16)] * 2,
            [(tall, F32), (volume, F32), (volume, F32), (tall, F32), (tall, F32)],
            10_000_000_000,
            base_left,
            base_right,
            western,
            eastern,
            left_mix,
            right_mix,
            sketch,
        )

    def lower():
        bulk_left, bulk_right = run(
            lower_kernel,
            [(wide, BF16)] * 2,
            [(volume, F32)] * 2,
            10_000_000_000,
            base_left,
            base_right,
            western,
            eastern,
            left_mix,
            right_mix,
        )
        return jnp.zeros(double, BF16), bulk_left, bulk_right

    following, bulk_left, bulk_right = lax.cond(leading, upper, lower)

    def lower_part():
        (result,) = run(
            lower_gradient,
            [(square, F32)],
            [(tall, F32), (volume, F32)],
            1_000_000_000,
            received,
            western,
            kept,
        )
        return result

    grad_lower = lax.cond(leading, lambda: jnp.zeros(square, F32), lower_part)
    grad_lower, following = lax.optimization_barrier((grad_lower, following))
    sent = lax.ppermute(following, "row", [(0, 1)])

    def end(kernel, basis):
        return run(
            kernel, [(tall, BF16)] * 2, [(tall, F32)], 1_000_000_000, bulk_left, bulk_right, basis
        )

    def upper_end():
        (result,) = run(
            upper_gradient,
            [(square, F32)],
            [(volume, F32)],
            1_000_000_000,
            received,
            eastern,
            kept,
        )
        return (result, *end(upper_end_kernel, following))

    def lower_end():
        return (grad_lower, *end(lower_end_kernel, sent))

    gradient, left_new, right_new = lax.cond(leading, upper_end, lower_end)
    gradient = gradient.reshape(bond, bond, bond, bond)
    gradient = gradient.transpose(1, 0, 3, 2).reshape(1, 1, 1, bond**4)
    gradient = jnp.where(selection, gradient * (bond / chi), 0.0)
    return (
        gradient,
        left_new.reshape(left_bounds.shape),
        right_new.reshape(right_bounds.shape),
    )


def solution(mesh):
    return jax.shard_map(
        local,
        mesh=mesh,
        in_specs=(
            P(("grp", "row"), "col", None, None, None),
            P(("grp", "row"), "col", None, None, None),
            P(("grp", "row"), "col", None, None),
            P(("grp", "row"), "col"),
            P(("grp", "col"), None, None, None),
            P(("grp", "col"), None, None, None),
            P(),
        ),
        out_specs=(
            P(("grp", "row"), "col", None, None),
            P(("grp", "row"), "col", None, None, None),
            P(("grp", "row"), "col", None, None, None),
        ),
        check_vma=False,
    )
```

```python
import jax
import jax.numpy as jnp
from jax import lax
from jax.experimental import pallas as pl
from jax.experimental.pallas import tpu as pltpu
from jax.sharding import PartitionSpec as P

HIGHEST = lax.Precision.HIGHEST
BLOCK = 8


def shift(value, axis, distance):
    count = lax.axis_size(axis)
    return lax.ppermute(value, axis, [(i, (i + distance) % count) for i in range(count)])


def dot(lhs, rhs, dims, precision=None):
    return lax.dot_general(
        lhs, rhs, (dims, ((), ())), precision=precision, preferred_element_type=jnp.float32
    )


def spread_row(value, row):
    return jnp.broadcast_to(value[row : row + 1, :], value.shape)


def eliminate_panel(rows, inverse, start):
    sublane = lax.broadcasted_iota(jnp.int32, rows.shape, 0)
    columns = [
        jnp.broadcast_to(rows[:, start + c : start + c + 1], rows.shape) for c in range(BLOCK)
    ]
    for c in range(BLOCK):
        scale = lax.rsqrt(spread_row(columns[c], c))
        factor = jnp.where(
            sublane > c, columns[c] * (scale * scale), jnp.where(sublane == c, 1.0 - scale, 0.0)
        )
        rows = rows - factor * spread_row(rows, c)
        inverse = inverse - factor * spread_row(inverse, c)
        for k in range(c + 1, BLOCK):
            columns[k] = columns[k] - factor * spread_row(columns[k], c)
    return rows, inverse


def inverse_factors(grams):
    size = grams[0].shape[0]
    ones = (
        lax.broadcasted_iota(jnp.int32, (size, size), 0)
        == lax.broadcasted_iota(jnp.int32, (size, size), 1)
    ).astype(jnp.float32)
    states = [jnp.concatenate([gram, ones], axis=1) for gram in grams]
    found = [[] for _ in grams]
    for start in range(0, size, BLOCK):
        for q in range(len(grams)):
            rows, inverse = eliminate_panel(
                states[q][:BLOCK, :size], states[q][:BLOCK, size:], start
            )
            found[q].append(inverse)
            if start + BLOCK < size:
                update = dot(
                    rows, jnp.concatenate([rows, inverse], axis=1), ((0,), (0,)), HIGHEST
                )
                states[q] = states[q][BLOCK:] - update[start + BLOCK :]
    return [jnp.concatenate(blocks, axis=0) for blocks in found]


def loop(count, step, start=0, unroll=4):
    def several(i, carry):
        for j in range(unroll):
            carry = step(i * unroll + j, carry)
        return carry

    return lax.fori_loop(0, count // unroll, several, start)


def row_block(i, size):
    return pl.ds(pl.multiple_of(i * size, size), size)


def gram_of(source, size):
    precision = HIGHEST if source.dtype == jnp.float32 else None

    def step(i, total):
        block = source[row_block(i, size), :]
        return total + dot(block, block, ((0,), (0,)), precision)

    start = jnp.zeros((size, size), jnp.float32)
    return loop(source.shape[0] // size, step, start, 8)


def apply_transposed(source, inverse, out):
    size = inverse.shape[0]
    if source.dtype == jnp.float32:

        def step(i, carry):
            block = dot(source[row_block(i, size), :], inverse, ((1,), (1,)), HIGHEST)
            out[row_block(i, size), :] = block.astype(jnp.bfloat16)
            return carry

    else:
        high = inverse.astype(jnp.bfloat16)
        rest = inverse - high.astype(jnp.float32)
        middle = rest.astype(jnp.bfloat16)
        low = (rest - middle.astype(jnp.float32)).astype(jnp.bfloat16)

        def step(i, carry):
            block = source[row_block(i, size), :]
            total = dot(block, low, ((1,), (1,)))
            total = total + dot(block, middle, ((1,), (1,)))
            total = total + dot(block, high, ((1,), (1,)))
            out[row_block(i, size), :] = total.astype(jnp.bfloat16)
            return carry

    loop(source.shape[0] // size, step, unroll=8)


BF16 = jnp.bfloat16
F32 = jnp.float32


def half(value):
    return value.astype(BF16)


def flat(ref):
    outer, inner, lane = ref.shape
    return ref.reshape(outer * inner, lane)


def split_legs(matrix, rows_ref, count):
    size = rows_ref.shape[0] // count
    rows_ref[...] = matrix.astype(jnp.float32)
    return [half(rows_ref[pl.ds(leg, size, stride=count), :]) for leg in range(count)]


def stack(planes, target):
    size = planes[0].shape[0]
    for i, plane in enumerate(planes):
        target[i * size : (i + 1) * size, :] = plane


def project(planes, boundary, target):
    size = planes.shape[1]
    count = planes.shape[0] // size
    rows = flat(target)

    def step(u, carry):
        product = dot(planes[row_block(u, size), :], boundary, ((0,), (0,)))
        for k in range(count):
            rows[pl.ds(u * count + k, size, stride=count * count), :] = product[
                :, k * size : (k + 1) * size
            ]
        return carry

    loop(count, step)


def pair_up(matrix, others, swap, target):
    outer, inner, lane = target.shape
    bond = matrix.shape[0] // outer
    dims = ((1,), (1,)) if swap else ((1,), (0,))
    left = matrix[...]

    def step(d, carry):
        product = dot(left, others[row_block(d, lane), :], dims)
        target[:, row_block(d, bond), :] = product.reshape(outer, bond, lane)
        return carry

    loop(bond, step)


def mix(weights, source, store):
    outer, inner, lane = source.shape
    rows = flat(source)
    group = 8

    def step(i, carry):
        blocks = []
        for j in range(group):
            begin = pl.multiple_of((i * group + j) * inner, inner)
            blocks.append(half(rows[pl.ds(begin, inner), :]))
        product = dot(weights, jnp.concatenate(blocks, axis=1), ((1,), (0,)))
        for j in range(group):
            store(i * group + j, product[:, j * lane : (j + 1) * lane])
        return carry

    loop(outer // group, step)


def store_natural(target):
    inner = target.shape[1]
    rows = flat(target)

    def store(index, block):
        rows[pl.ds(pl.multiple_of(index * inner, inner), inner), :] = block

    return store


def store_by_leg(target, bond):
    length = target.shape[0] * bond
    rows = flat(target)

    def store(index, block):
        for d in range(bond):
            begin = pl.multiple_of(d * length + index * bond, bond)
            rows[pl.ds(begin, bond), :] = block[d * bond : (d + 1) * bond]

    return store


def leg_block(source, d, bond):
    length = source.shape[0] * bond
    return half(flat(source)[row_block(d, length), :])


def joined(planes):
    return jnp.concatenate(planes, axis=1)


def edge_kernel(env_ref, left_out, right_out, rows_ref, left_ref, right_ref):
    size = env_ref.shape[1]
    planes = split_legs(env_ref[...], rows_ref, env_ref.shape[0] // size)
    stack(planes, left_ref)
    stack([plane.T for plane in planes], right_ref)
    inverses = inverse_factors([gram_of(left_ref, size), gram_of(right_ref, size)])
    apply_transposed(left_ref, inverses[0], left_out)
    apply_transposed(right_ref, inverses[1], right_out)


def upper_kernel(
    left_base, right_base, west_ref, east_ref, left_mix, right_mix, sketch_ref,
    next_ref, left_bulk, right_bulk, rows_ref, part_ref, absorbed_ref, left_sum, right_sum,
):
    size = west_ref.shape[1]
    bond = west_ref.shape[0] // size
    for base, boundary, weights, bulk, total in (
        (left_base, west_ref, left_mix, left_bulk, left_sum),
        (right_base, east_ref, right_mix, right_bulk, right_sum),
    ):
        project(base, joined(split_legs(boundary[...], rows_ref, bond)), part_ref)
        mix(weights[...], part_ref, store_by_leg(absorbed_ref, bond))

        def step(d, carry, bulk=bulk, total=total):
            block = leg_block(absorbed_ref, d, bond)
            bulk[d] = block
            total[row_block(d, size), :] = dot(block, sketch_ref[...], ((0,), (0,)))
            return carry

        loop(bond, step)
    inverses = inverse_factors([gram_of(left_sum, size), gram_of(right_sum, size)])
    length = left_sum.shape[0]
    apply_transposed(left_sum, inverses[0], next_ref.at[:length])
    apply_transposed(right_sum, inverses[1], next_ref.at[length:])


def lower_kernel(
    left_edge, right_edge, west_ref, east_ref, left_mix, right_mix,
    left_bulk, right_bulk, first_ref, mixed_ref,
):
    size = west_ref.shape[1]
    bond = west_ref.shape[0] // size
    steps = bond * bond
    for edge, boundary, weights, bulk in (
        (left_edge, west_ref, left_mix, left_bulk),
        (right_edge, east_ref, right_mix, right_bulk),
    ):
        pair_up(boundary, edge, False, first_ref)
        mix(weights[...], first_ref, store_natural(mixed_ref))

        def step(o, carry, bulk=bulk):
            for u in range(bond):
                bulk[o, u * size : (u + 1) * size, :] = half(
                    flat(mixed_ref)[pl.ds(u * bond + o, size, stride=steps), :]
                )
            return carry

        loop(bond, step)


def down_kernel(
    env_ref, west_ref, east_ref, weights, kept_ref, state_ref,
    rows_ref, planes_ref, first_ref, mixed_ref,
):
    size = west_ref.shape[1]
    bond = west_ref.shape[0] // size
    west = joined(split_legs(west_ref[...], rows_ref, bond))
    stack(split_legs(env_ref[...], rows_ref, bond), planes_ref)
    project(planes_ref, west, first_ref)
    mix(weights[...], first_ref, store_by_leg(mixed_ref, bond))
    kept_ref[...] = half(first_ref[...])

    def down(d, carry):
        block = leg_block(mixed_ref, d, bond)
        state_ref[row_block(d, size), :] = half(dot(block, east_ref[...], ((0,), (0,))))
        return carry

    loop(bond, down)


def up_kernel(
    env_ref, west_ref, east_ref, weights, kept_ref, state_ref,
    rows_ref, planes_ref, second_ref, mixed_ref,
):
    size = west_ref.shape[1]
    bond = west_ref.shape[0] // size
    west = joined(split_legs(west_ref[...], rows_ref, bond))
    stack(split_legs(env_ref[...], rows_ref, bond), planes_ref)
    pair_up(east_ref, planes_ref, True, second_ref)
    mix(weights[...], second_ref, store_natural(mixed_ref))
    kept_ref[...] = half(second_ref[...])

    def up(u, carry):
        low = joined(
            [
                half(flat(mixed_ref)[pl.ds(u * bond + k, size, stride=bond * bond), :])
                for k in range(bond)
            ]
        )
        state_ref[row_block(u, size), :] = half(dot(west, low, ((1,), (1,))))
        return carry

    loop(bond, up)


def upper_gradient(state_ref, east_ref, kept_ref, out_ref, volume_ref):
    pair_up(east_ref, state_ref, True, volume_ref)
    overlap(kept_ref, volume_ref, out_ref)


def lower_gradient(state_ref, west_ref, kept_ref, out_ref, rows_ref, volume_ref):
    bond = west_ref.shape[0] // west_ref.shape[1]
    project(state_ref, joined(split_legs(west_ref[...], rows_ref, bond)), volume_ref)
    overlap(volume_ref, kept_ref, out_ref)


def overlap(part_ref, key_ref, out_ref):
    outer, inner, lane = part_ref.shape
    group = 8

    def gather(ref, i):
        rows = flat(ref)
        return joined(
            [
                half(rows[pl.ds(pl.multiple_of((i * group + j) * inner, inner), inner), :])
                for j in range(group)
            ]
        )

    def step(i, total):
        return total + dot(gather(part_ref, i), gather(key_ref, i), ((1,), (1,)))

    out_ref[...] = lax.fori_loop(
        0, outer // group, step, jnp.zeros((inner, inner), jnp.float32)
    )


def upper_end_kernel(
    left_bulk, right_bulk, basis_ref, left_out, right_out, rows_ref
):
    for bulk, basis, out in (
        (left_bulk, basis_ref.at[: basis_ref.shape[0] // 2], left_out),
        (right_bulk, basis_ref.at[basis_ref.shape[0] // 2 :], right_out),
    ):
        bond, length, size = bulk.shape

        def step(i, total, bulk=bulk, basis=basis):
            rows = row_block(i, size)
            block = dot(
                joined([bulk[d, rows, :] for d in range(bond)]), basis[...], ((1,), (0,))
            )
            rows_ref[rows, :] = block
            return total + jnp.sum(block * block, axis=0, keepdims=True)

        scaled_out(loop(length // size, step, jnp.zeros((1, size)), 8), rows_ref, out)


def scaled_out(total, rows_ref, out):
    mean = jnp.sum(total, keepdims=True) * (1.0 / (rows_ref.shape[0] * rows_ref.shape[1]))
    out[...] = half(rows_ref[...] * lax.rsqrt(mean + 1e-06))


def lower_end_kernel(
    left_bulk, right_bulk, basis_ref, left_out, right_out, rows_ref
):
    for bulk, basis, out in (
        (left_bulk, basis_ref.at[: basis_ref.shape[0] // 2], left_out),
        (right_bulk, basis_ref.at[basis_ref.shape[0] // 2 :], right_out),
    ):
        bond, length, size = bulk.shape
        flipped = basis[...].T

        def step(o, total, bulk=bulk, flipped=flipped):
            block = dot(flipped, bulk[o], ((1,), (0,)))
            rows_ref[pl.ds(o, size, stride=bond), :] = block
            return total + jnp.sum(block * block, axis=0, keepdims=True)

        scaled_out(loop(bond, step, jnp.zeros((1, size)), 8), rows_ref, out)


def run(kernel, outs, scratch, flops, *args):
    in_vmem = pl.BlockSpec(memory_space=pltpu.VMEM)
    return pl.pallas_call(
        kernel,
        out_shape=tuple(jax.ShapeDtypeStruct(shape, kind) for shape, kind in outs),
        in_specs=[in_vmem] * len(args),
        out_specs=(in_vmem,) * len(outs),
        scratch_shapes=[pltpu.VMEM(shape, kind) for shape, kind in scratch],
        compiler_params=pltpu.CompilerParams(vmem_limit_bytes=48 * 1024 * 1024),
        cost_estimate=pl.CostEstimate(
            flops=flops, bytes_accessed=2_000_000, transcendentals=0
        ),
    )(*args)


def local(left_bounds, right_bounds, site_tensors, configuration, top_env, bottom_env, sketch):
    chi = left_bounds.shape[2]
    bond = left_bounds.shape[3]
    phys = site_tensors.shape[2]
    tall = (chi * bond, chi)
    wide = (bond, chi * bond, chi)
    double = (2 * chi * bond, chi)
    square = (bond * bond, bond * bond)
    volume = (chi, bond * bond, chi)
    row = lax.axis_index("row")
    leading = row == 0
    western = shift(left_bounds.reshape(tall), "col", 1)
    eastern = shift(right_bounds.reshape(tall), "col", -1)
    selection = (
        lax.broadcasted_iota(jnp.int32, (1, 1, phys, 1), 2) == configuration[:, :, None, None]
    )
    selected = jnp.sum(jnp.where(selection, site_tensors, jnp.zeros_like(site_tensors)), axis=2)
    core = selected.reshape(bond, bond, bond, bond)
    env = jnp.where(leading, top_env[0], bottom_env[0]).reshape(tall)
    base_left, base_right = run(
        edge_kernel,
        [(tall, BF16)] * 2,
        [(tall, F32), (tall, BF16), (tall, BF16)],
        10_000_000_000,
        env,
    )
    env, base_left = lax.optimization_barrier((env, base_left))
    left_mix, right_mix = (
        jnp.where(leading, core.transpose(above), core.transpose(below)).reshape(square)
        for above, below in (((3, 2, 1, 0), (1, 2, 3, 0)), ((3, 0, 1, 2), (1, 0, 3, 2)))
    )

    def first_pass(kernel, weights):
        return lambda: run(
            kernel,
            [(volume, BF16), (tall, BF16)],
            [(tall, F32), (tall, BF16), (volume, F32), (volume, F32)],
            10_000_000_000,
            env,
            western,
            eastern,
            weights,
        )

    kept, state = lax.cond(
        leading, first_pass(down_kernel, left_mix), first_pass(up_kernel, right_mix)
    )
    received = lax.ppermute(state, "row", [(0, 1), (1, 0)])

    def upper():
        return run(
            upper_kernel,
            [(double, BF16)] + [(wide, BF16)] * 2,
            [(tall, F32), (volume, F32), (volume, F32), (tall, F32), (tall, F32)],
            10_000_000_000,
            base_left,
            base_right,
            western,
            eastern,
            left_mix,
            right_mix,
            sketch,
        )

    def lower():
        bulk_left, bulk_right = run(
            lower_kernel,
            [(wide, BF16)] * 2,
            [(volume, F32)] * 2,
            10_000_000_000,
            base_left,
            base_right,
            western,
            eastern,
            left_mix,
            right_mix,
        )
        return jnp.zeros(double, BF16), bulk_left, bulk_right

    following, bulk_left, bulk_right = lax.cond(leading, upper, lower)

    def lower_part():
        (result,) = run(
            lower_gradient,
            [(square, F32)],
            [(tall, F32), (volume, F32)],
            1_000_000_000,
            received,
            western,
            kept,
        )
        return result

    grad_lower = lax.cond(leading, lambda: jnp.zeros(square, F32), lower_part)
    grad_lower, following = lax.optimization_barrier((grad_lower, following))
    sent = lax.ppermute(following, "row", [(0, 1)])

    def end(kernel, basis):
        return run(
            kernel, [(tall, BF16)] * 2, [(tall, F32)], 1_000_000_000, bulk_left, bulk_right, basis
        )

    def upper_end():
        (result,) = run(
            upper_gradient,
            [(square, F32)],
            [(volume, F32)],
            1_000_000_000,
            received,
            eastern,
            kept,
        )
        return (result, *end(upper_end_kernel, following))

    def lower_end():
        return (grad_lower, *end(lower_end_kernel, sent))

    gradient, left_new, right_new = lax.cond(leading, upper_end, lower_end)
    gradient = gradient.reshape(bond, bond, bond, bond)
    gradient = gradient.transpose(1, 0, 3, 2).reshape(1, 1, 1, bond**4)
    gradient = jnp.where(selection, gradient * (bond / chi), 0.0)
    return (
        gradient,
        left_new.reshape(left_bounds.shape),
        right_new.reshape(right_bounds.shape),
    )


def solution(mesh):
    return jax.shard_map(
        local,
        mesh=mesh,
        in_specs=(
            P(("grp", "row"), "col", None, None, None),
            P(("grp", "row"), "col", None, None, None),
            P(("grp", "row"), "col", None, None),
            P(("grp", "row"), "col"),
            P(("grp", "col"), None, None, None),
            P(("grp", "col"), None, None, None),
            P(),
        ),
        out_specs=(
            P(("grp", "row"), "col", None, None),
            P(("grp", "row"), "col", None, None, None),
            P(("grp", "row"), "col", None, None, None),
        ),
        check_vma=False,
    )
```
